32 devices in a mesh: tx: 4 (over z), cell: 8 (over y, x, core).
Axes of the slice: x: 2, y: 2, z: 4, core: 2. Of those that a mesh axis runs over, the one named last changes fastest.
Arguments:
- currents: bfloat16 [2, 2, 8192, 4096], P(None, None, 'cell', 'tx'), may hold values from -6 to 6
- green: bfloat16 [2, 2, 64, 8192], P(None, None, 'tx', 'cell'), may hold values from -0.0625 to 0.0625
- angular_freq: float32 [2], replicated, may hold values from 0.5 to 3
- gate_time: float32 [64], replicated, may hold values from 0.1 to 3
Outputs:
- gated: float32 [64, 64, 4096], P(None, 'cell', 'tx')
The draws below stay inside these ranges and needn't reach their ends.
All inputs are finite; a program needn't handle non-finite values.
Results may differ from the reference program's by a relative error of at most 0.0003.
Values may be sent and summed in bfloat16 or wider, within the bound.
No kernel may reach another device: no remote copies, remote signals or barrier semaphores. Data moves between devices by JAX's collectives and lax.ppermute only.
A program may use at most 128 MiB of HBM per device.

```python
import math
import jax
import jax.numpy as jnp
from jax import lax

FREQS = 2
GATES = 64
CELLS = 8192
TRANSMITTERS = 4096
RECEIVERS = 64


def strengthened(result, own_key, source, target, shards_of, factor):
    def block_of(axis_at):
        return (jnp.arange(result.shape[axis_at]) // (result.shape[axis_at] // shards_of)).reshape((-1,) + (1,) * (result.ndim - 1 - axis_at))

    near = jax.random.permutation(own_key, shards_of)[block_of(target)]
    far = (block_of(target) + shards_of // 2) % shards_of
    return jnp.where((block_of(source) == near) | (block_of(source) == far), factor * result, result)


def levels(stream_key, shape, split, low, largest):
    loudness = 1.0
    for dim, shards_of in split:
        draws = jax.random.uniform(jax.random.fold_in(jax.random.fold_in(stream_key, 6), dim), (shards_of,), jnp.float32, low / len(split), largest / len(split))
        loudness = loudness * jnp.repeat(jnp.exp(draws), shape[dim] // shards_of).reshape((-1,) + (1,) * (len(shape) - 1 - dim))
    return loudness


def gaussian(own_key, shape, deviation, reach, cuts=(), held_as=jnp.bfloat16):
    gain = levels(own_key, shape, cuts, -0.22, 0.18) if cuts else 1.0
    entries = jax.random.normal(own_key, shape, jnp.float32) * deviation * gain
    return jnp.minimum(jnp.maximum(entries, -reach), reach).astype(held_as)


def heavy_noise(stream_key, extent, width, most, pieces, heavy, kind=jnp.bfloat16):
    entries = width * jax.random.normal(stream_key, extent, jnp.float32)
    if pieces:
        entries = entries * levels(stream_key, extent, pieces, -0.22, 0.18)
    return jnp.clip(strengthened(entries, jax.random.fold_in(stream_key, 3), *heavy), -most, most).astype(kind)


def setup_inputs(seed: int = 0) -> dict:
    streams_of = jax.random.split(jax.random.key(seed), 5)
    return {
        "currents": gaussian(streams_of[0], (2, FREQS, CELLS, TRANSMITTERS), 1.0, 6.0, ((2, 8), (3, 4))),
        "green": heavy_noise(streams_of[1], (2, FREQS, RECEIVERS, CELLS), (2 * CELLS) ** -0.5, 0.0625, ((2, 4), (3, 8)), (3, 2, 8, 2.0)),
        "angular_freq": jnp.clip(jnp.exp(jax.random.uniform(streams_of[2], (FREQS,), jnp.float32, math.log(0.5), math.log(3.0))), 0.5, 3.0),
        "gate_time": jnp.clip(jnp.exp(jax.random.uniform(streams_of[3], (GATES,), jnp.float32, math.log(0.1), math.log(3.0))), 0.1, 3.0),
    }


def reference(currents, green, angular_freq, gate_time):
    real_list = []
    imag_list = []
    for which_freq in range(FREQS):
        green_real = green[0, which_freq]
        green_imag = green[1, which_freq]
        curr_real = currents[0, which_freq]
        curr_imag = currents[1, which_freq]
        real_list.append(jnp.dot(green_real, curr_real, preferred_element_type=jnp.float32)
                         - jnp.dot(green_imag, curr_imag, preferred_element_type=jnp.float32))
        imag_list.append(jnp.dot(green_real, curr_imag, preferred_element_type=jnp.float32)
                         + jnp.dot(green_imag, curr_real, preferred_element_type=jnp.float32))
    response_real = jnp.stack(real_list)
    response_imaginary = jnp.stack(imag_list)
    gate_phase = gate_time[:, None] * angular_freq[None, :]
    cosine_weight = jnp.cos(gate_phase)
    sine_weight = jnp.sin(gate_phase)
    gated = jnp.einsum("ks,seh->keh", cosine_weight, response_real, precision=lax.Precision.HIGHEST)
    gated = gated - jnp.einsum("ks,seh->keh", sine_weight, response_imaginary, precision=lax.Precision.HIGHEST)
    return gated
```

```python
import functools

import jax
import jax.numpy as jnp
from jax import lax
from jax.experimental import pallas as pl
from jax.experimental.pallas import tpu as pltpu
from jax.sharding import PartitionSpec as P

VMEM = pl.BlockSpec(memory_space=pltpu.VMEM)
SMEM = pl.BlockSpec(memory_space=pltpu.SMEM)
GATES_AT_ONCE = 8


def response_kernel(blocks, chips, place_ref, *refs):
    slots, currents_ref = refs[:blocks], refs[blocks]
    keep_ref, send_ref, straight_ref, crossed_ref = refs[blocks + 1 :]
    my_tx, my_chip, my_core = place_ref[0], place_ref[1], place_ref[2]
    freqs = currents_ref.shape[1]
    per_block = chips // blocks
    rows = slots[0].shape[2] // per_block
    half = rows // 2
    for f in range(freqs):
        for slot in range(blocks):
            block = lax.bitwise_xor(my_tx, slot)
            for j in range(per_block):
                chip = lax.bitwise_xor(block * per_block + j, my_chip)
                real = slots[slot][0, f, j * rows : (j + 1) * rows, :]
                imag = slots[slot][1, f, j * rows : (j + 1) * rows, :]
                straight_ref[f, 0, chip] = real
                straight_ref[f, 1, chip] = imag
                crossed_ref[f, 0, chip] = -imag
                crossed_ref[f, 1, chip] = real
    cells = currents_ref.shape[2]
    width = currents_ref.shape[3]
    step = min(width, 512)
    for f in range(freqs):
        straight = straight_ref[f].reshape(2 * chips * rows, cells)
        crossed = crossed_ref[f].reshape(2 * chips * rows, cells)
        for at in range(0, width, step):
            cols = slice(at, at + step)
            total = jnp.dot(straight, currents_ref[0, f, :, cols], preferred_element_type=jnp.float32)
            total += jnp.dot(crossed, currents_ref[1, f, :, cols], preferred_element_type=jnp.float32)
            total = total.reshape(2, chips, 2, half, step)
            first = my_core == 0
            for part in range(2):
                keep = jnp.where(first, total[part, :, 0], total[part, :, 1])
                send = jnp.where(first, total[part, :, 1], total[part, :, 0])
                keep_ref[:, f * 2 + part, :, cols] = keep
                send_ref[:, f * 2 + part, :, cols] = send


def responses(place, slots, currents, chips):
    _, freqs, block_rows, cells = slots[0].shape
    width = currents.shape[3]
    rows = block_rows * len(slots) // chips
    out = jax.ShapeDtypeStruct((chips, 2 * freqs, rows // 2, width), jnp.float32)
    products = pltpu.VMEM((freqs, 2, chips, rows, cells), jnp.bfloat16)
    return pl.pallas_call(
        functools.partial(response_kernel, len(slots), chips),
        out_shape=(out, out),
        in_specs=[SMEM] + [VMEM] * (len(slots) + 1),
        out_specs=(VMEM, VMEM),
        scratch_shapes=[products, products],
        compiler_params=pltpu.CompilerParams(vmem_limit_bytes=48 << 20),
        name="responses",
    )(place, *slots, currents)


def gate_kernel(parts, weight_ref, *refs):
    pieces, out_ref = refs[:parts], refs[parts]
    held_ref, sems = refs[parts + 1 :]
    terms = pieces[0].shape[0]
    gates = out_ref.shape[0]
    total = [sum(piece[t] for piece in pieces[1:]) + pieces[0][t] for t in range(terms)]
    copies = []
    for at in range(0, gates, GATES_AT_ONCE):
        for g in range(at, at + GATES_AT_ONCE):
            value = weight_ref[0, g] * total[0]
            for t in range(1, terms):
                value += weight_ref[t, g] * total[t]
            held_ref[g] = value
        group = pl.ds(at, GATES_AT_ONCE)
        copy = pltpu.make_async_copy(held_ref.at[group], out_ref.at[group], sems.at[at // GATES_AT_ONCE])
        copy.start()
        copies.append(copy)
    for copy in copies:
        copy.wait()


def gates_of(weights, pieces):
    terms, gates = weights.shape
    _, rows, width = pieces[0].shape
    return pl.pallas_call(
        functools.partial(gate_kernel, len(pieces)),
        out_shape=jax.ShapeDtypeStruct((gates, rows, width), jnp.float32),
        in_specs=[SMEM] + [VMEM] * len(pieces),
        out_specs=pl.BlockSpec(memory_space=pl.ANY),
        scratch_shapes=[
            pltpu.VMEM((gates, rows, width), jnp.float32),
            pltpu.SemaphoreType.DMA((gates // GATES_AT_ONCE,)),
        ],
        compiler_params=pltpu.CompilerParams(vmem_limit_bytes=32 << 20),
        name="gates",
    )(weights, *pieces)


def per_device(txs, cells, currents, green, angular_freq, gate_time):
    chips = cells // 2
    my_cell = lax.axis_index("cell")
    place = jnp.stack([lax.axis_index("tx"), my_cell // 2, my_cell % 2]).astype(jnp.int32)
    gate_phase = angular_freq[:, None] * gate_time[None, :]
    weights = jnp.stack([jnp.cos(gate_phase), -jnp.sin(gate_phase)], 1).reshape(-1, gate_time.shape[0])

    slots = [green] + [lax.ppermute(green, "tx", [(i, i ^ s) for i in range(txs)]) for s in range(1, txs)]
    keep, send = responses(place, slots, currents, chips)
    chip_sum = keep + lax.ppermute(send, "cell", [(i, i ^ 1) for i in range(cells)])
    pieces = [chip_sum[0]] + [
        lax.ppermute(chip_sum[k], "cell", [(i, i ^ (2 * k)) for i in range(cells)]) for k in range(1, chips)
    ]
    return gates_of(weights, pieces)


def solution(mesh):
    return jax.shard_map(
        functools.partial(per_device, mesh.shape["tx"], mesh.shape["cell"]),
        mesh=mesh,
        in_specs=(P(None, None, "cell", "tx"), P(None, None, "tx", "cell"), P(), P()),
        out_specs=P(None, "cell", "tx"),
        check_vma=False,
    )
```

```python
import functools

import jax
import jax.numpy as jnp
from jax import lax
from jax.experimental import pallas as pl
from jax.experimental.pallas import tpu as pltpu
from jax.sharding import PartitionSpec as P

VMEM = pl.BlockSpec(memory_space=pltpu.VMEM)
ANY = pl.BlockSpec(memory_space=pl.ANY)
GATES_AT_ONCE = 8
LANES = 128


def cost(flops, moved):
    return pl.CostEstimate(flops=flops, bytes_accessed=moved, transcendentals=0)


def fetch_kernel(currents_ref, green_ref, held_ref, own_ref, sems):
    copies = [
        pltpu.make_async_copy(currents_ref, held_ref, sems.at[0]),
        pltpu.make_async_copy(green_ref, own_ref, sems.at[1]),
    ]
    for copy in copies:
        copy.start()
    for copy in copies:
        copy.wait()


def fetch(currents, green):
    return pl.pallas_call(
        fetch_kernel,
        out_shape=(
            jax.ShapeDtypeStruct(currents.shape, currents.dtype),
            jax.ShapeDtypeStruct(green.shape, green.dtype),
        ),
        in_specs=[ANY, ANY],
        out_specs=(VMEM, VMEM),
        scratch_shapes=[pltpu.SemaphoreType.DMA((2,))],
        compiler_params=pltpu.CompilerParams(vmem_limit_bytes=16 << 20),
        cost_estimate=cost(0, 4 * currents.size),
        name="fetch",
    )(currents, green)


def response_kernel(offsets, chips, *refs):
    blocks = len(offsets)
    slots, currents_ref = refs[:blocks], refs[blocks]
    keep_ref, send_ref, straight_ref, crossed_ref = refs[blocks + 1 :]
    my_tx, my_cell = lax.axis_index("tx"), lax.axis_index("cell")
    my_chip, my_core = my_cell // 2, my_cell % 2
    _, freqs, cells, width = currents_ref.shape
    per_block = chips // blocks
    rows = straight_ref.shape[3]
    for f in range(freqs):
        for slot, offset in enumerate(offsets):
            block = lax.bitwise_xor(my_tx, offset)
            for j in range(per_block):
                chip = lax.bitwise_xor(block * per_block + j, my_chip)
                real = slots[slot][0, f, j * rows : (j + 1) * rows, :]
                imag = slots[slot][1, f, j * rows : (j + 1) * rows, :]
                straight_ref[f, 0, chip] = real
                straight_ref[f, 1, chip] = imag
                crossed_ref[f, 0, chip] = -imag
                crossed_ref[f, 1, chip] = real
    step = min(width, 512)
    first = my_core == 0
    for f in range(freqs):
        straight = straight_ref[f].reshape(2 * chips * rows, cells)
        crossed = crossed_ref[f].reshape(2 * chips * rows, cells)
        for at in range(0, width, step):
            cols = slice(at, at + step)
            total = jnp.dot(straight, currents_ref[0, f, :, cols], preferred_element_type=jnp.float32)
            total += jnp.dot(crossed, currents_ref[1, f, :, cols], preferred_element_type=jnp.float32)
            total = total.reshape(2, chips, 2, rows // 2, step)
            for part in range(2):
                here = 2 * f + part
                keep_ref[:, here, :, cols] = jnp.where(first, total[part, :, 0], total[part, :, 1])
                send_ref[:, here, :, cols] = jnp.where(first, total[part, :, 1], total[part, :, 0])


def responses(offsets, slots, currents, chips):
    _, freqs, block_rows, cells = slots[0].shape
    width = currents.shape[3]
    rows = block_rows * len(slots) // chips
    out = jax.ShapeDtypeStruct((chips, 2 * freqs, rows // 2, width), jnp.float32)
    products = pltpu.VMEM((freqs, 2, chips, rows, cells), jnp.bfloat16)
    return pl.pallas_call(
        functools.partial(response_kernel, offsets, chips),
        out_shape=(out, out),
        in_specs=[VMEM] * (len(slots) + 1),
        out_specs=(VMEM, VMEM),
        scratch_shapes=[products, products],
        compiler_params=pltpu.CompilerParams(vmem_limit_bytes=24 << 20),
        cost_estimate=cost(8 * freqs * chips * rows * cells * width, 4 * freqs * cells * width),
        name="responses",
    )(*slots, currents)


def gate_kernel(parts, weight_ref, *refs):
    pieces, out_ref = refs[:parts], refs[parts]
    held_ref, sems = refs[parts + 1 :]
    terms, rows, width = pieces[0].shape
    gates = out_ref.shape[0]
    blocks = [slice(at, at + LANES) for at in range(0, width, LANES)]
    total = []
    for t in range(terms):
        whole = sum(piece[t] for piece in pieces[1:]) + pieces[0][t]
        total.append([whole[:, block] for block in blocks])
    copies = []
    for at in range(0, gates, GATES_AT_ONCE):
        for g in range(at, at + GATES_AT_ONCE):
            weight = [jnp.broadcast_to(weight_ref[g, t : t + 1, :], (rows, LANES)) for t in range(terms)]
            for i, block in enumerate(blocks):
                value = weight[0] * total[0][i]
                for t in range(1, terms):
                    value += weight[t] * total[t][i]
                held_ref[g, :, block] = value
        group = pl.ds(at, GATES_AT_ONCE)
        copy = pltpu.make_async_copy(held_ref.at[group], out_ref.at[group], sems.at[at // GATES_AT_ONCE])
        copy.start()
        copies.append(copy)
    for copy in copies:
        copy.wait()


def gates_of(weights, pieces):
    gates = weights.shape[0]
    _, rows, width = pieces[0].shape
    return pl.pallas_call(
        functools.partial(gate_kernel, len(pieces)),
        out_shape=jax.ShapeDtypeStruct((gates, rows, width), jnp.float32),
        in_specs=[VMEM] * (1 + len(pieces)),
        out_specs=ANY,
        scratch_shapes=[
            pltpu.VMEM((gates, rows, width), jnp.float32),
            pltpu.SemaphoreType.DMA((gates // GATES_AT_ONCE,)),
        ],
        compiler_params=pltpu.CompilerParams(vmem_limit_bytes=24 << 20),
        name="gates",
    )(weights, *pieces)


def per_device(txs, cells, currents, green, angular_freq, gate_time):
    chips = cells // 2
    gate_phase = gate_time[:, None] * angular_freq[None, :]
    weights = jnp.stack([jnp.cos(gate_phase), -jnp.sin(gate_phase)], 2).reshape(gate_time.shape[0], -1)
    weights = jnp.broadcast_to(weights[:, :, None], weights.shape + (LANES,))

    offsets = sorted(range(1, txs), key=lambda s: (s != txs // 2, s))
    sent = [lax.ppermute(green, "tx", [(i, i ^ s) for i in range(txs)]) for s in offsets]
    held, own = fetch(currents, green)
    keep, send = responses([*offsets, 0], [*sent, own], held, chips)
    chip_sum = keep + lax.ppermute(send, "cell", [(i, i ^ 1) for i in range(cells)])
    pieces = [
        lax.ppermute(chip_sum[k], "cell", [(i, i ^ (2 * k)) for i in range(cells)]) for k in range(chips - 1, 0, -1)
    ]
    pieces.append(chip_sum[0])
    return gates_of(weights, pieces)


def solution(mesh):
    return jax.shard_map(
        functools.partial(per_device, mesh.shape["tx"], mesh.shape["cell"]),
        mesh=mesh,
        in_specs=(P(None, None, "cell", "tx"), P(None, None, "tx", "cell"), P(), P()),
        out_specs=P(None, "cell", "tx"),
        check_vma=False,
    )
```

```python
import functools

import jax
import jax.numpy as jnp
from jax import lax
from jax.experimental import pallas as pl
from jax.experimental.pallas import tpu as pltpu
from jax.sharding import PartitionSpec as P

VMEM = pl.BlockSpec(memory_space=pltpu.VMEM)
ANY = pl.BlockSpec(memory_space=pl.ANY)
GATES_AT_ONCE = 8
LANES = 128


def cost(flops, moved):
    return pl.CostEstimate(flops=flops, bytes_accessed=moved, transcendentals=0)


def response_kernel(freq, offsets, chips, *refs):
    blocks = len(offsets)
    slots, currents_ref = refs[:blocks], refs[blocks]
    keep_ref, send_ref, straight_ref, crossed_ref = refs[blocks + 1 :]
    my_tx, my_cell = lax.axis_index("tx"), lax.axis_index("cell")
    my_chip, my_core = my_cell // 2, my_cell % 2
    _, _, cells, width = currents_ref.shape
    per_block = chips // blocks
    rows = straight_ref.shape[2]
    for slot, offset in enumerate(offsets):
        block = lax.bitwise_xor(my_tx, offset)
        whole = len(slots[slot].shape) == 4
        for j in range(per_block):
            chip = lax.bitwise_xor(block * per_block + j, my_chip)
            here = slice(j * rows, (j + 1) * rows)
            real = slots[slot][0, freq, here, :] if whole else slots[slot][0, here, :]
            imag = slots[slot][1, freq, here, :] if whole else slots[slot][1, here, :]
            straight_ref[0, chip] = real
            straight_ref[1, chip] = imag
            crossed_ref[0, chip] = -imag
            crossed_ref[1, chip] = real
    step = min(width, 512)
    first = my_core == 0
    straight = straight_ref[...].reshape(2 * chips * rows, cells)
    crossed = crossed_ref[...].reshape(2 * chips * rows, cells)
    for at in range(0, width, step):
        cols = slice(at, at + step)
        total = jnp.dot(straight, currents_ref[0, freq, :, cols], preferred_element_type=jnp.float32)
        total += jnp.dot(crossed, currents_ref[1, freq, :, cols], preferred_element_type=jnp.float32)
        total = total.reshape(2, chips, 2, rows // 2, step)
        for part in range(2):
            keep_ref[:, part, :, cols] = jnp.where(first, total[part, :, 0], total[part, :, 1])
            send_ref[:, part, :, cols] = jnp.where(first, total[part, :, 1], total[part, :, 0])


def responses(freq, offsets, slots, currents, chips):
    _, _, cells, width = currents.shape
    rows = slots[0].shape[-2] * len(slots) // chips
    out = jax.ShapeDtypeStruct((chips, 2, rows // 2, width), jnp.float32)
    products = pltpu.VMEM((2, chips, rows, cells), jnp.bfloat16)
    return pl.pallas_call(
        functools.partial(response_kernel, freq, offsets, chips),
        out_shape=(out, out),
        in_specs=[VMEM] * (len(slots) + 1),
        out_specs=(VMEM, VMEM),
        scratch_shapes=[products, products],
        compiler_params=pltpu.CompilerParams(vmem_limit_bytes=16 << 20),
        cost_estimate=cost(8 * chips * rows * cells * width, 4 * cells * width),
        name="responses",
    )(*slots, currents)


def gate_kernel(parts, weight_ref, *refs):
    pieces, out_ref = refs[:parts], refs[parts]
    held_ref, sems = refs[parts + 1 :]
    terms, rows, width = pieces[0].shape
    gates = out_ref.shape[0]
    blocks = [slice(at, at + LANES) for at in range(0, width, LANES)]
    total = []
    for t in range(terms):
        whole = sum(piece[t] for piece in pieces[1:]) + pieces[0][t]
        total.append([whole[:, block] for block in blocks])
    copies = []
    for at in range(0, gates, GATES_AT_ONCE):
        for g in range(at, at + GATES_AT_ONCE):
            weight = [jnp.broadcast_to(weight_ref[g, t : t + 1, :], (rows, LANES)) for t in range(terms)]
            for i, block in enumerate(blocks):
                value = weight[0] * total[0][i]
                for t in range(1, terms):
                    value += weight[t] * total[t][i]
                held_ref[g, :, block] = value
        group = pl.ds(at, GATES_AT_ONCE)
        copy = pltpu.make_async_copy(held_ref.at[group], out_ref.at[group], sems.at[at // GATES_AT_ONCE])
        copy.start()
        copies.append(copy)
    for copy in copies:
        copy.wait()


def gates_of(weights, pieces):
    gates = weights.shape[0]
    _, rows, width = pieces[0].shape
    return pl.pallas_call(
        functools.partial(gate_kernel, len(pieces)),
        out_shape=jax.ShapeDtypeStruct((gates, rows, width), jnp.float32),
        in_specs=[VMEM] * (1 + len(pieces)),
        out_specs=ANY,
        scratch_shapes=[
            pltpu.VMEM((gates, rows, width), jnp.float32),
            pltpu.SemaphoreType.DMA((gates // GATES_AT_ONCE,)),
        ],
        compiler_params=pltpu.CompilerParams(vmem_limit_bytes=24 << 20),
        name="gates",
    )(weights, *pieces)


def lane_kernel(weight_ref, out_ref):
    out_ref[...] = jnp.broadcast_to(weight_ref[...][:, :, None], out_ref.shape)


def lane_copies(weights):
    return pl.pallas_call(
        lane_kernel,
        out_shape=jax.ShapeDtypeStruct(weights.shape + (LANES,), weights.dtype),
        in_specs=[VMEM],
        out_specs=VMEM,
        compiler_params=pltpu.CompilerParams(vmem_limit_bytes=8 << 20),
        cost_estimate=cost(4 << 30, 1 << 20),
        name="weights",
    )(weights)


def per_device(txs, cells, currents, green, angular_freq, gate_time):
    chips = cells // 2
    gate_phase = gate_time[:, None] * angular_freq[None, :]
    weights = lane_copies(jnp.stack([jnp.cos(gate_phase), -jnp.sin(gate_phase)], 2).reshape(gate_time.shape[0], -1))

    def swap(a, axis, bit):
        return lax.ppermute(a, axis, [(i, i ^ bit) for i in range({"tx": txs, "cell": cells}[axis])])

    freqs = currents.shape[1]
    own = [green[:, f] for f in range(freqs)]
    far = [swap(own[f], "tx", txs // 2) for f in range(freqs)]
    near = swap(lax.optimization_barrier((green, own[-1]))[0], "tx", 1)
    far[0], weights = lax.optimization_barrier((far[0], weights))
    keeps, gots = [], []
    for f in range(freqs):
        slots = {0: own[f], 1: near, txs // 2: far[f], txs // 2 + 1: swap(far[f], "tx", 1)}
        offsets = [txs // 2, 1, txs // 2 + 1, 0]
        keep, send = responses(f, offsets, [slots[s] for s in offsets], currents, chips)
        keeps.append(keep)
        gots.append(swap(send, "cell", 1))
    sums = jnp.concatenate([keep + got for keep, got in zip(keeps, gots)], 1)
    pieces = [swap(sums[k], "cell", 2 * k) for k in range(chips - 1, 0, -1)] + [sums[0]]
    return gates_of(weights, pieces)


def solution(mesh):
    return jax.shard_map(
        functools.partial(per_device, mesh.shape["tx"], mesh.shape["cell"]),
        mesh=mesh,
        in_specs=(P(None, None, "cell", "tx"), P(None, None, "tx", "cell"), P(), P()),
        out_specs=P(None, "cell", "tx"),
        check_vma=False,
    )
```

```python
import functools

import jax
import jax.numpy as jnp
from jax import lax
from jax.experimental import pallas as pl
from jax.experimental.pallas import tpu as pltpu
from jax.sharding import PartitionSpec as P

VMEM = pl.BlockSpec(memory_space=pltpu.VMEM)
ANY = pl.BlockSpec(memory_space=pl.ANY)
GATES_AT_ONCE = 8
LANES = 128


def cost(flops, moved):
    return pl.CostEstimate(flops=flops, bytes_accessed=moved, transcendentals=0)


def response_kernel(freq, offsets, chips, *refs):
    blocks = len(offsets)
    slots, currents_ref = refs[:blocks], refs[blocks]
    keep_ref, send_ref, straight_ref, crossed_ref = refs[blocks + 1 :]
    my_tx, my_cell = lax.axis_index("tx"), lax.axis_index("cell")
    my_chip, my_core = my_cell // 2, my_cell % 2
    _, _, cells, width = currents_ref.shape
    per_block = chips // blocks
    rows = straight_ref.shape[2]
    for slot, offset in enumerate(offsets):
        block = lax.bitwise_xor(my_tx, offset)
        whole = len(slots[slot].shape) == 4
        for j in range(per_block):
            chip = lax.bitwise_xor(block * per_block + j, my_chip)
            here = slice(j * rows, (j + 1) * rows)
            real = slots[slot][0, freq, here, :] if whole else slots[slot][0, here, :]
            imag = slots[slot][1, freq, here, :] if whole else slots[slot][1, here, :]
            straight_ref[0, chip] = real
            straight_ref[1, chip] = imag
            crossed_ref[0, chip] = -imag
            crossed_ref[1, chip] = real
    step = min(width, 512)
    first = my_core == 0
    straight = straight_ref[...].reshape(2 * chips * rows, cells)
    crossed = crossed_ref[...].reshape(2 * chips * rows, cells)
    for at in range(0, width, step):
        cols = slice(at, at + step)
        total = jnp.dot(straight, currents_ref[0, freq, :, cols], preferred_element_type=jnp.float32)
        total += jnp.dot(crossed, currents_ref[1, freq, :, cols], preferred_element_type=jnp.float32)
        total = total.reshape(2, chips, 2, rows // 2, step)
        for part in range(2):
            keep_ref[:, part, :, cols] = jnp.where(first, total[part, :, 0], total[part, :, 1])
            send_ref[:, part, :, cols] = jnp.where(first, total[part, :, 1], total[part, :, 0])


def responses(freq, offsets, slots, currents, chips):
    _, _, cells, width = currents.shape
    rows = slots[0].shape[-2] * len(slots) // chips
    out = jax.ShapeDtypeStruct((chips, 2, rows // 2, width), jnp.float32)
    products = pltpu.VMEM((2, chips, rows, cells), jnp.bfloat16)
    return pl.pallas_call(
        functools.partial(response_kernel, freq, offsets, chips),
        out_shape=(out, out),
        in_specs=[VMEM] * (len(slots) + 1),
        out_specs=(VMEM, VMEM),
        scratch_shapes=[products, products],
        compiler_params=pltpu.CompilerParams(vmem_limit_bytes=16 << 20),
        cost_estimate=cost(8 * chips * rows * cells * width, 4 * cells * width),
        name="responses",
    )(*slots, currents)


def gate_kernel(parts, weight_ref, *refs):
    pieces, out_ref = refs[:parts], refs[parts]
    held_ref, sems = refs[parts + 1 :]
    gates, terms, _ = weight_ref.shape
    _, rows, width = out_ref.shape
    blocks = [slice(at, at + LANES) for at in range(0, width, LANES)]
    whole = [piece for piece in pieces if piece.shape[0] == terms]
    split = [piece for piece in pieces if piece.shape[0] != terms]
    total = []
    for t in range(terms):
        value = sum(piece[t] for piece in whole)
        if split:
            value += split[t // 2][t % 2]
        total.append([value[:, block] for block in blocks])
    copies = []
    for at in range(0, gates, GATES_AT_ONCE):
        for g in range(at, at + GATES_AT_ONCE):
            weight = [jnp.broadcast_to(weight_ref[g, t : t + 1, :], (rows, LANES)) for t in range(terms)]
            for i, block in enumerate(blocks):
                value = weight[0] * total[0][i]
                for t in range(1, terms):
                    value += weight[t] * total[t][i]
                held_ref[g, :, block] = value
        group = pl.ds(at, GATES_AT_ONCE)
        copy = pltpu.make_async_copy(held_ref.at[group], out_ref.at[group], sems.at[at // GATES_AT_ONCE])
        copy.start()
        copies.append(copy)
    for copy in copies:
        copy.wait()


def gates_of(weights, pieces):
    gates = weights.shape[0]
    _, rows, width = pieces[0].shape
    return pl.pallas_call(
        functools.partial(gate_kernel, len(pieces)),
        out_shape=jax.ShapeDtypeStruct((gates, rows, width), jnp.float32),
        in_specs=[VMEM] * (1 + len(pieces)),
        out_specs=ANY,
        scratch_shapes=[
            pltpu.VMEM((gates, rows, width), jnp.float32),
            pltpu.SemaphoreType.DMA((gates // GATES_AT_ONCE,)),
        ],
        compiler_params=pltpu.CompilerParams(vmem_limit_bytes=24 << 20),
        name="gates",
    )(weights, *pieces)


def lane_kernel(weight_ref, out_ref):
    out_ref[...] = jnp.broadcast_to(weight_ref[...][:, :, None], out_ref.shape)


def lane_copies(weights):
    return pl.pallas_call(
        lane_kernel,
        out_shape=jax.ShapeDtypeStruct(weights.shape + (LANES,), weights.dtype),
        in_specs=[VMEM],
        out_specs=VMEM,
        compiler_params=pltpu.CompilerParams(vmem_limit_bytes=8 << 20),
        cost_estimate=cost(4 << 30, 1 << 20),
        name="weights",
    )(weights)


def per_device(txs, cells, currents, green, angular_freq, gate_time):
    chips = cells // 2
    gate_phase = gate_time[:, None] * angular_freq[None, :]
    weights = lane_copies(jnp.stack([jnp.cos(gate_phase), -jnp.sin(gate_phase)], 2).reshape(gate_time.shape[0], -1))

    def swap(a, axis, bit):
        return lax.ppermute(a, axis, [(i, i ^ bit) for i in range({"tx": txs, "cell": cells}[axis])])

    freqs = currents.shape[1]
    own = [green[:, f] for f in range(freqs)]
    far = [swap(own[f], "tx", txs // 2) for f in range(freqs)]
    near = swap(lax.optimization_barrier((green, own[-1]))[0], "tx", 1)
    far[0], weights = lax.optimization_barrier((far[0], weights))
    beyond = [swap(far[f], "tx", 1) for f in range(freqs)]
    sums, early = [], []
    last = chips - 1
    for f in range(freqs):
        slots = {0: own[f], 1: near, txs // 2: far[f], txs // 2 + 1: beyond[f]}
        offsets = [txs // 2, 1, txs // 2 + 1, 0]
        keep, send = responses(f, offsets, [slots[s] for s in offsets], currents, chips)
        if f:
            send, sums[-1] = lax.optimization_barrier((send, sums[-1]))
        size = chips if f == freqs - 1 else max(chips // 4, 1)
        got = [swap(send[at : at + size], "cell", 1) for at in range(0, chips, size)]
        sums.append(keep + jnp.concatenate(got))
    early = [swap(by_freq[last], "cell", 2 * last) for by_freq in sums]
    sums = jnp.concatenate([by_freq[:last] for by_freq in sums], 1)
    rest = [swap(sums[k], "cell", 2 * k) for k in range(1, last)] + [sums[0]]
    pieces = early[:1] + rest + early[1:]
    return gates_of(weights, pieces)


def solution(mesh):
    return jax.shard_map(
        functools.partial(per_device, mesh.shape["tx"], mesh.shape["cell"]),
        mesh=mesh,
        in_specs=(P(None, None, "cell", "tx"), P(None, None, "tx", "cell"), P(), P()),
        out_specs=P(None, "cell", "tx"),
        check_vma=False,
    )
```

```python
import functools

import jax
import jax.numpy as jnp
from jax import lax
from jax.experimental import pallas as pl
from jax.experimental.pallas import tpu as pltpu
from jax.sharding import PartitionSpec as P

VMEM = pl.BlockSpec(memory_space=pltpu.VMEM)
ANY = pl.BlockSpec(memory_space=pl.ANY)
GATES_AT_ONCE = 8
LANES = 128


def cost(flops, moved):
    return pl.CostEstimate(flops=flops, bytes_accessed=moved, transcendentals=0)


def response_kernel(freq, offsets, chips, *refs):
    blocks = len(offsets)
    slots, currents_ref = refs[:blocks], refs[blocks]
    keep_ref, send_ref, straight_ref, crossed_ref = refs[blocks + 1 :]
    my_tx, my_cell = lax.axis_index("tx"), lax.axis_index("cell")
    my_chip, my_core = my_cell // 2, my_cell % 2
    _, _, cells, width = currents_ref.shape
    per_block = chips // blocks
    rows = straight_ref.shape[2]
    for slot, offset in enumerate(offsets):
        block = lax.bitwise_xor(my_tx, offset)
        whole = len(slots[slot].shape) == 4
        for j in range(per_block):
            chip = lax.bitwise_xor(block * per_block + j, my_chip)
            here = slice(j * rows, (j + 1) * rows)
            real = slots[slot][0, freq, here, :] if whole else slots[slot][0, here, :]
            imag = slots[slot][1, freq, here, :] if whole else slots[slot][1, here, :]
            straight_ref[0, chip] = real
            straight_ref[1, chip] = imag
            crossed_ref[0, chip] = -imag
            crossed_ref[1, chip] = real
    step = min(width, 512)
    first = my_core == 0
    straight = straight_ref[...].reshape(2 * chips * rows, cells)
    crossed = crossed_ref[...].reshape(2 * chips * rows, cells)
    for at in range(0, width, step):
        cols = slice(at, at + step)
        total = jnp.dot(straight, currents_ref[0, freq, :, cols], preferred_element_type=jnp.float32)
        total += jnp.dot(crossed, currents_ref[1, freq, :, cols], preferred_element_type=jnp.float32)
        total = total.reshape(2, chips, 2, rows // 2, step)
        for part in range(2):
            keep_ref[:, part, :, cols] = jnp.where(first, total[part, :, 0], total[part, :, 1])
            send_ref[:, part, :, cols] = jnp.where(first, total[part, :, 1], total[part, :, 0])


def responses(freq, offsets, slots, currents, chips):
    _, _, cells, width = currents.shape
    rows = slots[0].shape[-2] * len(slots) // chips
    out = jax.ShapeDtypeStruct((chips, 2, rows // 2, width), jnp.float32)
    products = pltpu.VMEM((2, chips, rows, cells), jnp.bfloat16)
    return pl.pallas_call(
        functools.partial(response_kernel, freq, offsets, chips),
        out_shape=(out, out),
        in_specs=[VMEM] * (len(slots) + 1),
        out_specs=(VMEM, VMEM),
        scratch_shapes=[products, products],
        compiler_params=pltpu.CompilerParams(vmem_limit_bytes=16 << 20),
        cost_estimate=cost(8 * chips * rows * cells * width, 4 * cells * width),
        name="responses",
    )(*slots, currents)


def gate_kernel(parts, weight_ref, *refs):
    pieces, out_ref = refs[:parts], refs[parts]
    held_ref, sems = refs[parts + 1 :]
    gates, terms, _ = weight_ref.shape
    _, rows, width = out_ref.shape
    blocks = [slice(at, at + LANES) for at in range(0, width, LANES)]
    whole = [piece for piece in pieces if piece.shape[0] == terms]
    split = [piece for piece in pieces if piece.shape[0] != terms]
    total = []
    for t in range(terms):
        value = sum(piece[t] for piece in whole)
        if split:
            value += split[t // 2][t % 2]
        total.append([value[:, block] for block in blocks])
    copies = []
    for at in range(0, gates, GATES_AT_ONCE):
        for g in range(at, at + GATES_AT_ONCE):
            weight = [jnp.broadcast_to(weight_ref[g, t : t + 1, :], (rows, LANES)) for t in range(terms)]
            for i, block in enumerate(blocks):
                value = weight[0] * total[0][i]
                for t in range(1, terms):
                    value += weight[t] * total[t][i]
                held_ref[g, :, block] = value
        group = pl.ds(at, GATES_AT_ONCE)
        copy = pltpu.make_async_copy(held_ref.at[group], out_ref.at[group], sems.at[at // GATES_AT_ONCE])
        copy.start()
        copies.append(copy)
    for copy in copies:
        copy.wait()


def gates_of(weights, pieces):
    gates = weights.shape[0]
    _, rows, width = pieces[0].shape
    return pl.pallas_call(
        functools.partial(gate_kernel, len(pieces)),
        out_shape=jax.ShapeDtypeStruct((gates, rows, width), jnp.float32),
        in_specs=[VMEM] * (1 + len(pieces)),
        out_specs=ANY,
        scratch_shapes=[
            pltpu.VMEM((gates, rows, width), jnp.float32),
            pltpu.SemaphoreType.DMA((gates // GATES_AT_ONCE,)),
        ],
        compiler_params=pltpu.CompilerParams(vmem_limit_bytes=24 << 20),
        name="gates",
    )(weights, *pieces)


def lane_kernel(weight_ref, out_ref):
    out_ref[...] = jnp.broadcast_to(weight_ref[...][:, :, None], out_ref.shape)


def lane_copies(weights):
    return pl.pallas_call(
        lane_kernel,
        out_shape=jax.ShapeDtypeStruct(weights.shape + (LANES,), weights.dtype),
        in_specs=[VMEM],
        out_specs=VMEM,
        compiler_params=pltpu.CompilerParams(vmem_limit_bytes=8 << 20),
        cost_estimate=cost(4 << 30, 1 << 20),
        name="weights",
    )(weights)


def per_device(txs, cells, currents, green, angular_freq, gate_time):
    chips = cells // 2
    gate_phase = gate_time[:, None] * angular_freq[None, :]
    weights = lane_copies(jnp.stack([jnp.cos(gate_phase), -jnp.sin(gate_phase)], 2).reshape(gate_time.shape[0], -1))

    def swap(a, axis, bit):
        return lax.ppermute(a, axis, [(i, i ^ bit) for i in range({"tx": txs, "cell": cells}[axis])])

    freqs = currents.shape[1]
    own = [green[:, f] for f in range(freqs)]
    far = [swap(own[f], "tx", txs // 2) for f in range(freqs)]
    near = swap(lax.optimization_barrier((green, own[-1]))[0], "tx", 1)
    far[0], weights = lax.optimization_barrier((far[0], weights))
    beyond = [swap(far[f], "tx", 1) for f in range(freqs)]
    sums, early = [], []
    last = chips - 1
    offsets = [txs // 2, 1, txs // 2 + 1, 0]
    for f in range(freqs):
        slots = {0: own[f], 1: near, txs // 2: far[f], txs // 2 + 1: beyond[f]}
        keep, send = responses(f, offsets, [slots[s] for s in offsets], currents, chips)
        if f < freqs - 1:
            size = max(chips // 4, 1)
            got = [swap(send[at : min(at + size, last)], "cell", 1) for at in range(0, last, size)]
            early.append(keep[last] + swap(send[last], "cell", 1))
            sums.append(keep[:last] + jnp.concatenate(got))
        else:
            whole = keep + swap(send, "cell", 1)
            early.append(whole[last])
            sums.append(whole[:last])
    early = [swap(farthest, "cell", 2 * last) for farthest in early]
    sums = jnp.concatenate(sums, 1)
    rest = [swap(sums[k], "cell", 2 * k) for k in range(1, last)] + [sums[0]]
    pieces = early[:1] + rest + early[1:]
    return gates_of(weights, pieces)


def solution(mesh):
    return jax.shard_map(
        functools.partial(per_device, mesh.shape["tx"], mesh.shape["cell"]),
        mesh=mesh,
        in_specs=(P(None, None, "cell", "tx"), P(None, None, "tx", "cell"), P(), P()),
        out_specs=P(None, "cell", "tx"),
        check_vma=False,
    )
```

```python
import functools

import jax
import jax.numpy as jnp
from jax import lax
from jax.experimental import pallas as pl
from jax.experimental.pallas import tpu as pltpu
from jax.sharding import PartitionSpec as P

VMEM = pl.BlockSpec(memory_space=pltpu.VMEM)
ANY = pl.BlockSpec(memory_space=pl.ANY)
GATES_AT_ONCE = 8
LANES = 128


def cost(flops, moved):
    return pl.CostEstimate(flops=flops, bytes_accessed=moved, transcendentals=0)


def response_kernel(freq, offsets, chips, *refs):
    blocks = len(offsets)
    slots, currents_ref = refs[:blocks], refs[blocks]
    keep_ref, send_ref, straight_ref, crossed_ref = refs[blocks + 1 :]
    my_tx, my_cell = lax.axis_index("tx"), lax.axis_index("cell")
    my_chip, my_core = my_cell // 2, my_cell % 2
    _, _, cells, width = currents_ref.shape
    per_block = chips // blocks
    rows = straight_ref.shape[2]
    for slot, offset in enumerate(offsets):
        block = lax.bitwise_xor(my_tx, offset)
        whole = len(slots[slot].shape) == 4
        for j in range(per_block):
            chip = lax.bitwise_xor(block * per_block + j, my_chip)
            here = slice(j * rows, (j + 1) * rows)
            real = slots[slot][0, freq, here, :] if whole else slots[slot][0, here, :]
            imag = slots[slot][1, freq, here, :] if whole else slots[slot][1, here, :]
            straight_ref[0, chip] = real
            straight_ref[1, chip] = imag
            crossed_ref[0, chip] = -imag
            crossed_ref[1, chip] = real
    step = min(width, 512)
    first = my_core == 0
    straight = straight_ref[...].reshape(2 * chips * rows, cells)
    crossed = crossed_ref[...].reshape(2 * chips * rows, cells)
    for at in range(0, width, step):
        cols = slice(at, at + step)
        total = jnp.dot(straight, currents_ref[0, freq, :, cols], preferred_element_type=jnp.float32)
        total += jnp.dot(crossed, currents_ref[1, freq, :, cols], preferred_element_type=jnp.float32)
        total = total.reshape(2, chips, 2, rows // 2, step)
        for part in range(2):
            keep_ref[:, part, :, cols] = jnp.where(first, total[part, :, 0], total[part, :, 1])
            send_ref[:, part, :, cols] = jnp.where(first, total[part, :, 1], total[part, :, 0])


def responses(freq, offsets, slots, currents, chips):
    _, _, cells, width = currents.shape
    rows = slots[0].shape[-2] * len(slots) // chips
    out = jax.ShapeDtypeStruct((chips, 2, rows // 2, width), jnp.float32)
    products = pltpu.VMEM((2, chips, rows, cells), jnp.bfloat16)
    return pl.pallas_call(
        functools.partial(response_kernel, freq, offsets, chips),
        out_shape=(out, out),
        in_specs=[VMEM] * (len(slots) + 1),
        out_specs=(VMEM, VMEM),
        scratch_shapes=[products, products],
        compiler_params=pltpu.CompilerParams(vmem_limit_bytes=16 << 20),
        cost_estimate=cost(8 * chips * rows * cells * width, 4 * cells * width),
        name="responses",
    )(*slots, currents)


def gate_kernel(parts, weight_ref, *refs):
    pieces, out_ref = refs[:parts], refs[parts]
    held_ref, sems = refs[parts + 1 :]
    gates, terms, _ = weight_ref.shape
    _, rows, width = out_ref.shape
    blocks = [slice(at, at + LANES) for at in range(0, width, LANES)]
    whole = [piece for piece in pieces if piece.shape[0] == terms]
    split = [piece for piece in pieces if piece.shape[0] != terms]
    total = []
    for t in range(terms):
        value = sum(piece[t] for piece in whole)
        if split:
            value += split[t // 2][t % 2]
        total.append([value[:, block] for block in blocks])
    copies = []
    for at in range(0, gates, GATES_AT_ONCE):
        for g in range(at, at + GATES_AT_ONCE):
            weight = [jnp.broadcast_to(weight_ref[g, t : t + 1, :], (rows, LANES)) for t in range(terms)]
            for i, block in enumerate(blocks):
                value = weight[0] * total[0][i]
                for t in range(1, terms):
                    value += weight[t] * total[t][i]
                held_ref[g, :, block] = value
        group = pl.ds(at, GATES_AT_ONCE)
        copy = pltpu.make_async_copy(held_ref.at[group], out_ref.at[group], sems.at[at // GATES_AT_ONCE])
        copy.start()
        copies.append(copy)
    for copy in copies:
        copy.wait()


def gates_of(weights, pieces):
    gates = weights.shape[0]
    _, rows, width = pieces[0].shape
    return pl.pallas_call(
        functools.partial(gate_kernel, len(pieces)),
        out_shape=jax.ShapeDtypeStruct((gates, rows, width), jnp.float32),
        in_specs=[VMEM] * (1 + len(pieces)),
        out_specs=ANY,
        scratch_shapes=[
            pltpu.VMEM((gates, rows, width), jnp.float32),
            pltpu.SemaphoreType.DMA((gates // GATES_AT_ONCE,)),
        ],
        compiler_params=pltpu.CompilerParams(vmem_limit_bytes=24 << 20),
        name="gates",
    )(weights, *pieces)


def lane_kernel(weight_ref, out_ref):
    out_ref[...] = jnp.broadcast_to(weight_ref[...][:, :, None], out_ref.shape)


def lane_copies(weights):
    return pl.pallas_call(
        lane_kernel,
        out_shape=jax.ShapeDtypeStruct(weights.shape + (LANES,), weights.dtype),
        in_specs=[VMEM],
        out_specs=VMEM,
        compiler_params=pltpu.CompilerParams(vmem_limit_bytes=8 << 20),
        cost_estimate=cost(4 << 30, 1 << 20),
        name="weights",
    )(weights)


def per_device(txs, cells, currents, green, angular_freq, gate_time):
    chips = cells // 2
    gate_phase = gate_time[:, None] * angular_freq[None, :]
    weights = lane_copies(jnp.stack([jnp.cos(gate_phase), -jnp.sin(gate_phase)], 2).reshape(gate_time.shape[0], -1))

    def swap(a, axis, bit):
        return lax.ppermute(a, axis, [(i, i ^ bit) for i in range({"tx": txs, "cell": cells}[axis])])

    freqs = currents.shape[1]
    far, near = swap(green, "tx", txs // 2), swap(green, "tx", 1)
    own = [green[:, f] for f in range(freqs)]
    weights, *own = lax.optimization_barrier((weights, *own))
    beyond = [swap(own[f], "tx", txs // 2 + 1) for f in range(freqs)]
    sums, early = [], []
    last = chips - 1
    offsets = [txs // 2, 1, txs // 2 + 1, 0]
    for f in range(freqs):
        slots = {0: green, 1: near, txs // 2: far, txs // 2 + 1: beyond[f]}
        keep, send = responses(f, offsets, [slots[s] for s in offsets], currents, chips)
        if f < freqs - 1:
            others = swap(send[:last], "cell", 1)
            early.append(keep[last] + swap(send[last], "cell", 1))
            sums.append(keep[:last] + others)
        else:
            whole = keep + swap(send, "cell", 1)
            early.append(whole[last])
            sums.append(whole[:last])
    early = [swap(farthest, "cell", 2 * last) for farthest in early]
    sums = jnp.concatenate(sums, 1)
    rest = [swap(sums[k], "cell", 2 * k) for k in range(1, last)] + [sums[0]]
    pieces = early[:1] + rest + early[1:]
    return gates_of(weights, pieces)


def solution(mesh):
    return jax.shard_map(
        functools.partial(per_device, mesh.shape["tx"], mesh.shape["cell"]),
        mesh=mesh,
        in_specs=(P(None, None, "cell", "tx"), P(None, None, "tx", "cell"), P(), P()),
        out_specs=P(None, "cell", "tx"),
        check_vma=False,
    )
```
